32 devices in a mesh: aa: 8 (over y, x, core), ba: 4 (over z).
Axes of the slice: x: 2, y: 2, z: 4, core: 2. Of those that a mesh axis runs over, the one named last changes fastest.
Arguments:
- amplitudes: bfloat16 [1024, 2048], P('ba', 'aa'), may hold values from -6 to 6
- integrals: bfloat16 [512, 512, 2048], P('aa', 'ba'), may hold values from -0.125 to 0.125
- virt_energy: float32 [512], replicated, may hold values from 0.2 to 2
- pair_energy: float32 [1024], replicated, may hold values from 0.3 to 3
Outputs:
- update: float32 [512, 512, 1024], P('aa', 'ba')
The draws below stay inside these ranges and needn't reach their ends.
All inputs are finite; a program needn't handle non-finite values.
Results may differ from the reference program's by a relative error of at most 0.0003.
Values may be sent and summed in bfloat16 or wider, within the bound.
A program may use at most 128 MiB of HBM per device.

```python
import math
import jax
import jax.numpy as jnp
from jax import lax

NV = 512
K = 2048
P_SIZE = 1024


def steps_of(own_key, shape, split, low, high):
    gain, own = 1.0, jax.random.fold_in(own_key, 6)
    for axis_at, blocks in split:
        draws = jnp.exp(jax.random.uniform(jax.random.fold_in(own, axis_at), (blocks,), jnp.float32, low / len(split), high / len(split)))
        gain = gain * jnp.repeat(draws, shape[axis_at] // blocks).reshape([-1 if axis == axis_at else 1 for axis in range(len(shape))])
    return gain


def scatter_about(rng, extent, deviation, bound, split=(), kind=jnp.bfloat16):
    result = jax.random.normal(rng, extent, jnp.float32) * deviation
    if len(split) > 0:
        result = steps_of(rng, extent, split, -0.22, 0.18) * result
    return jnp.clip(result, min=-bound, max=bound).astype(kind)


def setup_inputs(seed: int = 0) -> dict:
    key_of = jax.random.split(jax.random.key(seed), 5)
    return {
        "amplitudes": scatter_about(key_of[0], (P_SIZE, K), 1.0, 6.0, ((0, 4), (1, 8))),
        "integrals": scatter_about(key_of[1], (NV, NV, K), K ** -0.5, 0.125, ((0, 8), (1, 4))),
        "virt_energy": jnp.clip(jnp.exp(jax.random.uniform(key_of[2], (NV,), jnp.float32, math.log(0.2), math.log(2.0))), 0.2, 2.0),
        "pair_energy": jnp.clip(jnp.exp(jax.random.uniform(key_of[3], (P_SIZE,), jnp.float32, math.log(0.3), math.log(3.0))), 0.3, 3.0),
    }


def reference(amplitudes, integrals, virt_energy, pair_energy):
    flat = integrals.reshape(NV * NV, K)
    ladder = lax.dot_general(flat, amplitudes, (((1,), (1,)), ((), ())), preferred_element_type=jnp.float32)
    ladder = ladder.reshape(NV, NV, P_SIZE)
    denom = virt_energy[:, None, None] + virt_energy[None, :, None] + pair_energy[None, None, :]
    return ladder / denom
```

```python
import functools

import jax
import jax.numpy as jnp
from jax import lax
from jax.experimental import pallas as pl
from jax.experimental.pallas import tpu as pltpu
from jax.sharding import PartitionSpec as P

MESH = pl.DeviceIdType.MESH
CORES, SIDE = 2, 2
EARLY, SEGMENTS = 3, 8
GROUP, COLUMNS = 8, 2


def contract(left, right):
    return lax.dot_general(
        left, right, (((1,), (1,)), ((), ())), preferred_element_type=jnp.float32
    )


def pick(index, options):
    total = jnp.int32(0)
    for value, option in enumerate(options):
        total = total + jnp.where(index == value, jnp.int32(option), jnp.int32(0))
    return total


def gather_kernel(nb, early_rows, amp_ref, ints_ref, whole_ref, part_ref,
                  whole, ints, acc, recv_sem, send_sem, part_sem, load_sem, out_sem):
    a, b = lax.axis_index("aa"), lax.axis_index("ba")
    rows, cols = amp_ref.shape
    wide = CORES * cols
    groups, group_rows = ints_ref.shape[0], ints_ref.shape[1]
    late_rows = group_rows - early_rows
    core, chip = a % CORES, a // CORES
    x, y = chip % SIDE, chip // SIDE
    chips = [chip, y * SIDE + (1 - x), (1 - y) * SIDE + x, (1 - y) * SIDE + (1 - x)]
    partner = chip * CORES + (1 - core)
    x_dev, y_dev = chips[1] * CORES + core, chips[2] * CORES + core
    tables = [sorted(range(nb), key=lambda v: (abs(v - own), v)) for own in range(nb)]
    order = [b] + [pick(b, [tables[own][k] for own in range(nb)]) for k in range(1, nb)]
    up, down = b + 1, b - 1

    def load(q):
        span = pl.ds(pl.multiple_of(chips[q] * wide, wide), wide)
        return pltpu.make_async_copy(
            ints_ref.at[:, pl.ds(late_rows, early_rows), span], ints.at[q], load_sem.at[q]
        )

    for q in range(4):
        load(q).start()

    barrier = pltpu.get_barrier_semaphore()
    for dev in (partner, x_dev, y_dev):
        pl.semaphore_signal(barrier, inc=1, device_id=(dev, b), device_id_type=MESH)

    @pl.when(up < nb)
    def _():
        pl.semaphore_signal(barrier, inc=1, device_id=(a, up), device_id_type=MESH)

    @pl.when(down >= 0)
    def _():
        pl.semaphore_signal(barrier, inc=1, device_id=(a, down), device_id_type=MESH)

    peers = 3 + jnp.where(up < nb, 1, 0) + jnp.where(down >= 0, 1, 0)
    pl.semaphore_wait(barrier, peers)

    def slot(q, c, k):
        row = pl.ds(pl.multiple_of(order[k] * rows, rows), rows)
        col = pl.ds(pl.multiple_of(chips[q] * wide + c * cols, cols), cols)
        return whole.at[row, col]

    def remote(q, k, kind, dev, src=None):
        place = slot(q, core, k)
        sem = recv_sem.at[(chips[q] * CORES + core) * nb + order[k]]
        return pltpu.make_async_remote_copy(
            src_ref=place if src is None else src, dst_ref=place,
            send_sem=send_sem.at[kind * nb + k], recv_sem=sem,
            device_id=dev, device_id_type=MESH,
        )

    def arrived(q, c, k):
        place = slot(q, c, k)
        sem = recv_sem.at[(chips[q] * CORES + c) * nb + order[k]]
        pltpu.make_async_copy(place, place, sem).wait()

    def along(k):
        if k == 0:
            return [(0, up < nb, (a, up)), (9, down >= 0, (a, down))]
        below = order[k] < b
        return [(0, below & (up < nb), (a, up)), (9, (order[k] > b) & (down >= 0), (a, down))]

    def sends(q, k):
        found = [(1 + q, (partner, b))]
        if q == 0:
            found += [(5, (x_dev, b)), (6, (y_dev, b))]
        if q == 1 and k % 2 == 0:
            found += [(7, (y_dev, b))]
        if q == 2 and k % 2 == 1:
            found += [(8, (x_dev, b))]
        return found

    def forward(q, k, src=None):
        if q == 0:
            for kind, cond, dev in along(k):
                @pl.when(cond)
                def _():
                    remote(q, k, kind, dev, src).start()
            for kind, dev in reversed(sends(q, k)):
                remote(q, k, kind, dev, src).start()
        else:
            for kind, dev in reversed(sends(q, k)):
                remote(q, k, kind, dev, src).start()

    def multiply(q, k, first):
        row = pl.ds(pl.multiple_of(order[k] * rows, rows), rows)
        col = pl.ds(pl.multiple_of(chips[q] * wide, wide), wide)
        right = whole[row, col]

        def body(g, carry):
            left = ints[q, pl.ds(g * GROUP, GROUP)].reshape(GROUP * early_rows, wide)
            value = contract(left, right)
            place = pl.ds(g * GROUP * early_rows, GROUP * early_rows)
            acc[k, place] = value if first else acc[k, place] + value
            return carry

        lax.fori_loop(0, groups // GROUP, body, 0)

    forward(0, 0, amp_ref)
    mine = pltpu.make_async_copy(amp_ref, slot(0, core, 0), part_sem.at[0])
    mine.start()
    mine.wait()

    stages = [[(0, 0)]]
    for s in range(1, nb + 3):
        stage = [(0, s)] if s < nb else []
        if s - 1 < nb:
            stage += [(1, s - 1), (2, s - 1)]
        if 2 <= s and s - 2 < nb:
            stage += [(3, s - 2)]
        stages.append(stage)
    loaded, done = set(), {k: 0 for k in range(nb)}

    def partner_ready(stage):
        for q, k in stage:
            arrived(q, 1 - core, k)

    def product(q, k):
        if q not in loaded:
            load(q).wait()
            loaded.add(q)
        multiply(q, k, done[k] == 0)
        done[k] += 1
        if done[k] == 4:
            out_copy(k).start()

    def out_copy(k):
        col = pl.ds(pl.multiple_of(order[k] * rows, rows), rows)
        return pltpu.make_async_copy(acc.at[k], part_ref.at[:, col], out_sem.at[k])

    def whole_copy(k):
        row = pl.ds(pl.multiple_of(order[k] * rows, rows), rows)
        return pltpu.make_async_copy(whole.at[row], whole_ref.at[row], part_sem.at[1 + k])

    flat = []
    for s in range(len(stages) + 1):
        now = stages[s] if s < len(stages) else []
        before = stages[s - 1] if s > 0 else []
        if s > 0:
            for q, k in now:
                arrived(q, core, k)
                forward(q, k)
        for q, k in before:
            arrived(q, 1 - core, k)
        for q, k in before:
            product(q, k)
        for q, k in before:
            if q == 3:
                whole_copy(k).start()

    for k in range(nb):
        for kind, cond, dev in along(k):
            @pl.when(cond)
            def _():
                remote(0, k, kind, dev).wait_send()
        for q in range(4):
            for kind, dev in sends(q, k):
                remote(q, k, kind, dev).wait_send()
    for k in range(nb):
        whole_copy(k).wait()
        out_copy(k).wait()


def rest_kernel(late_rows, second, first_ref, second_ref, pair_ref, whole_ref, ints_ref, part_ref, out_ref):
    step = pl.program_id(0)
    group_rows = out_ref.shape[0]
    size = group_rows // SEGMENTS
    per_first = second // size
    width = out_ref.shape[1] // COLUMNS
    for c in range(COLUMNS):
        cols = pl.ds(c * width, width)
        value = contract(ints_ref[...], whole_ref[cols, :])
        for s in range(SEGMENTS):
            low = s * size
            fst = first_ref[step * (group_rows // second) + s // per_first]
            snd = second_ref[pl.ds((s % per_first) * size, size), :]
            denom = (fst + snd) + pair_ref[:, cols]
            top = value[low:low + size] if low < late_rows else part_ref[pl.ds(low - late_rows, size), cols]
            out_ref[pl.ds(low, size), cols] = top * pl.reciprocal(denom)


def overlapped(nb, amplitudes, integrals, first_energy, second_energy, pair_energy):
    first_count, second_count, cd_count = integrals.shape
    rows, cols = amplitudes.shape
    pairs = rows * nb
    total = first_count * second_count
    group_rows = 4 * second_count
    groups = total // group_rows
    early = group_rows * EARLY // SEGMENTS
    late = group_rows - early
    grouped = integrals.reshape(groups, group_rows, cd_count)
    sends = 10 * nb
    whole, part = pl.pallas_call(
        functools.partial(gather_kernel, nb, early),
        out_shape=(
            jax.ShapeDtypeStruct((pairs, cd_count), amplitudes.dtype),
            jax.ShapeDtypeStruct((groups * early, pairs), jnp.float32),
        ),
        in_specs=[pl.BlockSpec(memory_space=pltpu.VMEM), pl.BlockSpec(memory_space=pl.ANY)],
        out_specs=(pl.BlockSpec(memory_space=pl.ANY), pl.BlockSpec(memory_space=pl.ANY)),
        scratch_shapes=[
            pltpu.VMEM((pairs, cd_count), amplitudes.dtype),
            pltpu.VMEM((4, groups, early, CORES * cols), integrals.dtype),
            pltpu.VMEM((nb, groups * early, rows), jnp.float32),
            pltpu.SemaphoreType.DMA((4 * CORES * nb,)),
            pltpu.SemaphoreType.DMA((sends,)),
            pltpu.SemaphoreType.DMA((1 + nb,)),
            pltpu.SemaphoreType.DMA((4,)),
            pltpu.SemaphoreType.DMA((nb,)),
        ],
        compiler_params=pltpu.CompilerParams(
            collective_id=0, has_side_effects=True, vmem_limit_bytes=60 * 2**20
        ),
        name="gather_and_start",
    )(amplitudes, grouped)
    out = pl.pallas_call(
        functools.partial(rest_kernel, late, second_count),
        grid=(groups,),
        out_shape=jax.ShapeDtypeStruct((total, pairs), jnp.float32),
        in_specs=[
            pl.BlockSpec(memory_space=pltpu.SMEM),
            pl.BlockSpec((second_count, 1), lambda i: (0, 0)),
            pl.BlockSpec((1, pairs), lambda i: (0, 0)),
            pl.BlockSpec((pairs, cd_count), lambda i: (0, 0), pipeline_mode=pl.Buffered(1)),
            pl.BlockSpec((None, late, cd_count), lambda i: (i, 0, 0)),
            pl.BlockSpec((early, pairs), lambda i: (i, 0)),
        ],
        out_specs=pl.BlockSpec((group_rows, pairs), lambda i: (i, 0)),
        compiler_params=pltpu.CompilerParams(vmem_limit_bytes=60 * 2**20),
        name="finish",
    )(first_energy, second_energy[:, None], pair_energy[None, :], whole, grouped, part)
    return out.reshape(first_count, second_count, pairs)


def on_device(na, nb, amplitudes, integrals, virt_energy, pair_energy):
    first_count, second_count, cd_count = integrals.shape
    first_energy = lax.dynamic_slice_in_dim(
        virt_energy, lax.axis_index("aa") * first_count, first_count, 0
    )
    second_energy = lax.dynamic_slice_in_dim(
        virt_energy, lax.axis_index("ba") * second_count, second_count, 0
    )
    rows, cols = amplitudes.shape
    fits = na == CORES * SIDE * SIDE and rows % 128 == 0 and cols % 128 == 0
    if fits and first_count % (4 * GROUP) == 0 and second_count % 128 == 0:
        return overlapped(nb, amplitudes, integrals, first_energy, second_energy, pair_energy)
    flat_ints = integrals.reshape(first_count * second_count, cd_count)
    all_rows = lax.all_gather(amplitudes, "ba", axis=0, tiled=True)
    whole = lax.all_gather(all_rows, "aa", axis=1, tiled=True)
    ladder = contract(flat_ints, whole).reshape(first_count, second_count, -1)
    denom = first_energy[:, None, None] + second_energy[None, :, None] + pair_energy[None, None, :]
    return ladder / denom


def solution(mesh):
    placed = (P("ba", "aa"), P("aa", "ba", None), P(), P())
    body = functools.partial(on_device, mesh.shape["aa"], mesh.shape["ba"])
    return jax.shard_map(
        body, mesh=mesh, in_specs=placed, out_specs=P("aa", "ba", None), check_vma=False
    )
```
